256 devices in a mesh: seq: 16 (over z, y_hi), roll: 16 (over y_lo, x, core).
Axes of the slice: x: 4, y: 4 (y_hi: 2, y_lo: 2; y = y_hi * 2 + y_lo), z: 8, core: 2. Of those that a mesh axis runs over, the one named last changes fastest.
Arguments:
- tokens: int32 [16, 7936], P('roll', 'seq'), may hold values from 0 to 29
- breaks: int32 [16, 7936], P('roll', 'seq'), may hold values 0 or 1
- lengths: int32 [16], P('roll'), may hold values from 3968 to 7936, as said below
- embed_table: float32 [30, 1280], replicated, may hold values from -6 to 6
- break_vec: float32 [1280], replicated, may hold values from -6 to 6
- gain_in: float32 [2, 1280], replicated, may hold values from 0.25 to 1.75
- gain_mid: float32 [2, 640], replicated, may hold values from 0.25 to 1.75
- gain_out: float32 [2, 640], replicated, may hold values from 0.25 to 1.75
- w_in: bfloat16 [2, 1280, 640], P(None, 'roll'), may hold values from -0.15625 to 0.15625
- convolution_weight: bfloat16 [2, 640, 3200], P(None, 'roll'), may hold values from -0.109375 to 0.109375
- w_out: bfloat16 [2, 640, 1280], P(None, 'roll'), may hold values from -0.25 to 0.25
Outputs:
- encoded: bfloat16 [16, 7936, 1280], P('roll', 'seq')
The draws below stay inside these ranges and needn't reach their ends.
Inputs may be any that keep to these rules, and one draw needn't show every extreme that they name: `lengths`: some complex has all 7936 residues valid in every draw.
All inputs are finite; a program needn't handle non-finite values. No bound on the sum of `breaks` on one device may be relied on, other than what follows from the above.
Results may differ from the reference program's by a relative error of at most 0.014.
Values may be sent and summed in bfloat16 or wider, within the bound.
A program may use at most 64 MiB of HBM per device.

```python
import jax
import jax.numpy as jnp
from jax import lax

D = 1280
H = 640
KERNEL = 5
VOCAB = 30
BLOCKS = 2
BASE_DILATION = 64
LENGTH = 7936
COMPLEXES = 16


def draw_lengths(key, part):
    sampled = jax.random.randint(key, (COMPLEXES,), LENGTH // 2, LENGTH + 1)
    return sampled.at[0].set(LENGTH).astype(jnp.int32)


def touch_ends(array, key, least, top_value):
    extent = array.shape
    index_at = [jax.random.randint(jax.random.fold_in(key, axis), (), 0, extent[axis]) for axis in range(len(extent))]
    array = array.at[tuple(index_at)].set(least)
    longest = extent.index(max(extent))
    index_at[longest] = (index_at[longest] + 1) % extent[longest]
    return array.at[tuple(index_at)].set(top_value)


def steps_of(stream_key, extent, cuts, least, top_value):
    level = 1.0
    for axis_at, shards_of in cuts:
        steps = jax.random.uniform(jax.random.fold_in(jax.random.fold_in(stream_key, 6), axis_at), (shards_of,), jnp.float32, least / len(cuts), top_value / len(cuts))
        level = level * jnp.repeat(jnp.exp(steps), extent[axis_at] // shards_of).reshape((-1,) + (1,) * (len(extent) - 1 - axis_at))
    return level


def bell_draw(own_key, dims, deviation, most, shards=(), held_as=jnp.bfloat16):
    array = deviation * jax.random.normal(own_key, dims, jnp.float32)
    if shards:
        array = array * steps_of(own_key, dims, shards, -0.22, 0.18)
    return jnp.clip(array, -most, most).astype(held_as)


def setup_inputs(seed: int = 0) -> dict:
    keys = jax.random.split(jax.random.key(seed), 12)
    return {
        "tokens": touch_ends(jax.random.randint(keys[0], (COMPLEXES, LENGTH), 0, VOCAB), jax.random.fold_in(keys[0], 1), 0, VOCAB - 1).astype(jnp.int32),
        "breaks": touch_ends((jax.random.randint(keys[1], (COMPLEXES, LENGTH), 0, 32) < 1).astype(jnp.int32), jax.random.fold_in(keys[1], 1), 0, 1),
        "lengths": draw_lengths(jax.random.fold_in(keys[11], 71), 0),
        "embed_table": bell_draw(keys[3], (VOCAB, D), 1.0, 6.0, (), jnp.float32),
        "break_vec": bell_draw(keys[4], (D,), 1.0, 6.0, (), jnp.float32),
        "gain_in": jnp.clip(1.0 + 0.15 * jax.random.normal(keys[5], (BLOCKS, D), jnp.float32), 0.25, 1.75),
        "gain_mid": jnp.clip(1.0 + 0.15 * jax.random.normal(keys[6], (BLOCKS, H), jnp.float32), 0.25, 1.75),
        "gain_out": jnp.clip(1.0 + 0.15 * jax.random.normal(keys[7], (BLOCKS, H), jnp.float32), 0.25, 1.75),
        "w_in": bell_draw(keys[8], (BLOCKS, D, H), D ** -0.5, 0.15625, ((1, 16),)),
        "convolution_weight": bell_draw(keys[9], (BLOCKS, H, KERNEL * H), (KERNEL * H) ** -0.5, 0.109375, ((1, 16),)),
        "w_out": bell_draw(keys[10], (BLOCKS, H, D), H ** -0.5, 0.25, ((1, 16),)),
    }


def layer_norm(values, gain):
    center = lax.optimization_barrier(jnp.mean(values, axis=-1, keepdims=True))
    spread = lax.optimization_barrier(jnp.mean((values - center) ** 2, axis=-1, keepdims=True))
    return (values - center) * lax.rsqrt(spread + 1e-05) * gain

def reference(tokens, breaks, lengths, embed_table, break_vec, gain_in, gain_mid, gain_out, w_in, convolution_weight, w_out):

    def score_complex(items):
        token_row, boundary_row, length = items
        onehot = (token_row[:, None] == jnp.arange(VOCAB, dtype=jnp.int32)[None, :]).astype(jnp.float32)
        hidden_state = jnp.dot(onehot, embed_table, precision=lax.Precision.HIGHEST, preferred_element_type=jnp.float32)
        hidden_state = (hidden_state + boundary_row[:, None].astype(jnp.float32) * break_vec[None, :]).astype(jnp.bfloat16)
        position = jnp.arange(LENGTH, dtype=jnp.int32)
        valid_rows = (position < length).astype(jnp.float32)[:, None]
        for block_number in range(BLOCKS):
            dilation_step = BASE_DILATION * 2 ** block_number
            reach_rows = KERNEL // 2 * dilation_step
            normed = jax.nn.gelu(layer_norm(hidden_state.astype(jnp.float32), gain_in[block_number]), approximate=False).astype(jnp.bfloat16)
            padded_hidden = jnp.dot(normed, w_in[block_number], preferred_element_type=jnp.float32)
            conv_input = (jax.nn.gelu(layer_norm(padded_hidden, gain_mid[block_number]), approximate=False) * valid_rows).astype(jnp.bfloat16)
            padded = jnp.pad(conv_input, ((reach_rows, reach_rows), (0, 0)))
            taps_weight = convolution_weight[block_number].reshape(H, KERNEL, H)
            mixed = jnp.zeros((LENGTH, H), jnp.float32)
            for tap in range(KERNEL):
                window = padded[tap * dilation_step:tap * dilation_step + LENGTH]
                mixed = mixed + jnp.dot(window, taps_weight[:, tap, :], preferred_element_type=jnp.float32)
            activated = jax.nn.gelu(layer_norm(mixed, gain_out[block_number]), approximate=False).astype(jnp.bfloat16)
            hidden_state = (hidden_state.astype(jnp.float32) + jnp.dot(activated, w_out[block_number], preferred_element_type=jnp.float32)).astype(jnp.bfloat16)
        return hidden_state
    return lax.map(score_complex, (tokens, breaks, lengths))
```

```python
import jax
import jax.numpy as jnp
from jax import lax
from jax.sharding import Mesh, PartitionSpec as P

H = 640
KERNEL = 5
VOCAB = 30
BLOCKS = 2
BASE_DILATION = 64
ROLL = ("ylo", "x", "core")


def extended_2(x, sides, width):
    for axis, dim in sides:
        size, length = (lax.axis_size(axis), x.shape[dim])
        up = [(i, (i + 1) % size) for i in range(size - 1)]
        down = [(j, i) for i, j in up]
        last = lax.slice_in_dim(x, length - width, length, axis=dim)
        initial = lax.slice_in_dim(x, 0, width, axis=dim)
        before = lax.ppermute(last, axis, up)
        after = lax.ppermute(initial, axis, down)
        x = jnp.concatenate([before, x, after], axis=dim)
    return x


def layer_norm(values, gain):
    center = jnp.mean(values, axis=-1, keepdims=True)
    spread = jnp.mean((values - center) ** 2, axis=-1, keepdims=True)
    return (values - center) * lax.rsqrt(spread + 1e-05) * gain


def pack_block(w_in, conv, w_out):
    k_mid = conv.shape[0]
    conv_rows = conv.reshape(k_mid, KERNEL, H).transpose(1, 0, 2).reshape(KERNEL * k_mid, H)
    halves = w_out.shape[1] // H
    out_rows = w_out.reshape(k_mid, halves, H).transpose(1, 0, 2).reshape(halves * k_mid, H)
    return jnp.concatenate([w_in, conv_rows, out_rows], axis=0)


def per_device(
    tokens,
    breaks,
    lengths,
    embed_table,
    break_vec,
    gain_in,
    gain_mid,
    gain_out,
    w_in,
    convolution_weight,
    w_out,
):
    local_rows = tokens.shape[1]
    complexes = tokens.shape[0]
    seq_place = lax.axis_index("seq")
    k_in = w_in.shape[1]
    k_mid = convolution_weight.shape[1]
    d_model = w_out.shape[2]
    halves = d_model // H
    block_rows = k_in + KERNEL * k_mid + halves * k_mid

    packed = jnp.concatenate(
        [pack_block(w_in[b], convolution_weight[b], w_out[b]) for b in range(BLOCKS)], axis=0
    )
    gathered = lax.all_gather(packed, ("ylo", "x"), axis=0, tiled=False)
    gathered = lax.all_gather(gathered, "core", axis=0, tiled=False)
    n_core = gathered.shape[0]
    n_chip = gathered.shape[1]

    onehot = (tokens[:, :, None] == jnp.arange(VOCAB, dtype=jnp.int32)[None, None, :]).astype(
        jnp.float32
    )
    hidden_state = jnp.einsum(
        "cnv,vd->cnd",
        onehot,
        embed_table,
        precision=lax.Precision.HIGHEST,
        preferred_element_type=jnp.float32,
    )
    hidden_state = (
        hidden_state + breaks[:, :, None].astype(jnp.float32) * break_vec[None, None, :]
    ).astype(jnp.bfloat16)
    position = seq_place * local_rows + jnp.arange(local_rows, dtype=jnp.int32)
    valid_rows = ((position[None, :] >= 0) & (position[None, :] < lengths[:, None])).astype(
        jnp.float32
    )
    for block_number in range(BLOCKS):
        dilation_step = BASE_DILATION * 2**block_number
        reach_rows = KERNEL // 2 * dilation_step
        base = block_number * block_rows
        in_w = gathered[:, :, base : base + k_in, :]
        normed = jax.nn.gelu(
            layer_norm(hidden_state.astype(jnp.float32), gain_in[block_number]), approximate=False
        ).astype(jnp.bfloat16)
        normed4 = normed.reshape(complexes, local_rows, n_chip, n_core, k_in)
        padded_hidden = jnp.einsum(
            "cnaqj,qajh->cnh", normed4, in_w, preferred_element_type=jnp.float32
        )
        conv_input = (
            jax.nn.gelu(layer_norm(padded_hidden, gain_mid[block_number]), approximate=False)
            * valid_rows[:, :, None]
        ).astype(jnp.bfloat16)
        extended = extended_2(conv_input, (("seq", 1),), reach_rows)
        mixed = jnp.zeros((complexes, local_rows, H), jnp.float32)
        for tap in range(KERNEL):
            start = base + k_in + tap * k_mid
            tap_w = gathered[:, :, start : start + k_mid, :]
            window = extended[:, tap * dilation_step : tap * dilation_step + local_rows]
            window4 = window.reshape(complexes, local_rows, n_chip, n_core, k_mid)
            mixed = mixed + jnp.einsum(
                "cnaql,qalo->cno", window4, tap_w, preferred_element_type=jnp.float32
            )
        activated = jax.nn.gelu(
            layer_norm(mixed, gain_out[block_number]), approximate=False
        ).astype(jnp.bfloat16)
        start = base + k_in + KERNEL * k_mid
        out_w = gathered[:, :, start : start + halves * k_mid, :].reshape(
            n_core, n_chip, halves, k_mid, H
        )
        act4 = activated.reshape(complexes, local_rows, n_chip, n_core, k_mid)
        update = jnp.einsum(
            "cnaql,qahlo->cnho", act4, out_w, preferred_element_type=jnp.float32
        ).reshape(complexes, local_rows, d_model)
        hidden_state = (hidden_state.astype(jnp.float32) + update).astype(jnp.bfloat16)
    return hidden_state


def solution(mesh):
    seq_size, roll_size = mesh.devices.shape
    devices = mesh.devices.reshape(seq_size, roll_size // 8, 4, 2)
    fine = Mesh(devices, ("seq",) + ROLL)
    placed = (
        P(ROLL, "seq"),
        P(ROLL, "seq"),
        P(ROLL),
        P(),
        P(),
        P(),
        P(),
        P(),
        P(None, ROLL, None),
        P(None, ROLL, None),
        P(None, ROLL, None),
    )
    return jax.shard_map(
        per_device, mesh=fine, in_specs=placed, out_specs=P(ROLL, "seq", None), check_vma=False
    )
```

```python
import jax
import jax.numpy as jnp
from jax import lax
from jax.experimental import pallas as pl
from jax.experimental.pallas import tpu as pltpu
from jax.sharding import Mesh, PartitionSpec as P

H = 640
KERNEL = 5
VOCAB = 30
BLOCKS = 2
BASE_DILATION = 64
ROLL = ("ylo", "x", "core")
MESH = pl.DeviceIdType.MESH


def extended_2(x, sides, width):
    for axis, dim in sides:
        size, length = (lax.axis_size(axis), x.shape[dim])
        up = [(i, (i + 1) % size) for i in range(size - 1)]
        down = [(j, i) for i, j in up]
        last = lax.slice_in_dim(x, length - width, length, axis=dim)
        initial = lax.slice_in_dim(x, 0, width, axis=dim)
        before = lax.ppermute(last, axis, up)
        after = lax.ppermute(initial, axis, down)
        x = jnp.concatenate([before, x, after], axis=dim)
    return x


def layer_norm(values, gain):
    center = jnp.mean(values, axis=-1, keepdims=True)
    spread = jnp.mean((values - center) ** 2, axis=-1, keepdims=True)
    return (values - center) * lax.rsqrt(spread + 1e-05) * gain


def gather_kernel(in_ref, out_ref, send_sem, recv_sem, local_sem):
    n_x = lax.axis_size("x")
    seq_i = lax.axis_index("seq")
    ylo = lax.axis_index("ylo")
    x = lax.axis_index("x")
    c = lax.axis_index("core")
    z = seq_i // 2
    y = (seq_i % 2) * 2 + ylo
    other = 1 - ylo

    def slot(par, xx, cc):
        return (par * n_x + xx) * 2 + cc

    def y_dev(yy):
        return (z * 2 + yy // 2, yy % 2, x, c)

    x_right = lax.rem(x + 1, n_x)
    x_left = lax.rem(x + n_x - 1, n_x)
    x_far = lax.rem(x + 2, n_x)
    right = (seq_i, ylo, x_right, c)
    left = (seq_i, ylo, x_left, c)
    up = y_dev(lax.rem(y + 1, 4))
    down = y_dev(lax.rem(y + 3, 4))
    partner = (seq_i, ylo, x, 1 - c)

    barrier = pltpu.get_barrier_semaphore()
    for dev in (right, left, up, down, partner):
        pl.semaphore_signal(barrier, inc=1, device_id=dev, device_id_type=MESH)
    pl.semaphore_wait(barrier, 5)

    sends = []

    def send(src, s, h, dev):
        cp = pltpu.make_async_remote_copy(
            src_ref=src,
            dst_ref=out_ref.at[s, h],
            send_sem=send_sem.at[len(sends)],
            recv_sem=recv_sem.at[s, h],
            device_id=dev,
            device_id_type=MESH,
        )
        cp.start()
        sends.append(cp)

    def arrive(s, h, dev):
        pltpu.make_async_remote_copy(
            src_ref=out_ref.at[s, h],
            dst_ref=out_ref.at[s, h],
            send_sem=send_sem.at[0],
            recv_sem=recv_sem.at[s, h],
            device_id=dev,
            device_id_type=MESH,
        ).wait_recv()

    me = slot(ylo, x, c)
    for h in range(2):
        send(in_ref.at[h], me, h, right)
    for h in range(2):
        send(in_ref.at[h], me, h, left)
    send(in_ref.at[0], me, 0, up)
    send(in_ref.at[1], me, 1, down)
    for h in range(2):
        send(in_ref.at[h], me, h, partner)
    locals_ = []
    for h in range(2):
        cp = pltpu.make_async_copy(in_ref.at[h], out_ref.at[me, h], local_sem.at[h])
        cp.start()
        locals_.append(cp)

    s_left = slot(ylo, x_left, c)
    s_right = slot(ylo, x_right, c)
    for h in range(2):
        arrive(s_left, h, left)
    send(out_ref.at[s_left, 0], s_left, 0, right)
    send(out_ref.at[s_left, 0], s_left, 0, up)
    send(out_ref.at[s_left, 1], s_left, 1, down)
    for h in range(2):
        arrive(s_right, h, right)
    send(out_ref.at[s_right, 1], s_right, 1, left)
    send(out_ref.at[s_right, 0], s_right, 0, up)
    send(out_ref.at[s_right, 1], s_right, 1, down)
    for s in (s_left, s_right):
        for h in range(2):
            send(out_ref.at[s, h], s, h, partner)

    s_far = slot(ylo, x_far, c)
    arrive(s_far, 0, left)
    arrive(s_far, 1, right)
    send(out_ref.at[s_far, 0], s_far, 0, up)
    send(out_ref.at[s_far, 1], s_far, 1, down)
    for h in range(2):
        send(out_ref.at[s_far, h], s_far, h, partner)

    for xx in (x, x_left, x_right, x_far):
        s = slot(other, xx, c)
        arrive(s, 0, down)
        arrive(s, 1, up)
        for h in range(2):
            send(out_ref.at[s, h], s, h, partner)

    for par in (ylo, other):
        for xx in (x, x_left, x_right, x_far):
            s = slot(par, xx, 1 - c)
            for h in range(2):
                arrive(s, h, partner)
    for cp in sends:
        cp.wait_send()
    for cp in locals_:
        cp.wait()


def gather_weights(packed, n_slots):
    return pl.pallas_call(
        gather_kernel,
        out_shape=jax.ShapeDtypeStruct((n_slots,) + packed.shape, packed.dtype),
        in_specs=[pl.BlockSpec(memory_space=pl.ANY)],
        out_specs=pl.BlockSpec(memory_space=pl.ANY),
        scratch_shapes=[
            pltpu.SemaphoreType.DMA((32,)),
            pltpu.SemaphoreType.DMA((n_slots, 2)),
            pltpu.SemaphoreType.DMA((2,)),
        ],
        compiler_params=pltpu.CompilerParams(collective_id=0, has_side_effects=True),
    )(packed)


def pack_block(w_in, conv, w_out):
    k_mid = conv.shape[0]
    conv_rows = conv.reshape(k_mid, KERNEL, H).transpose(1, 0, 2).reshape(KERNEL * k_mid, H)
    halves = w_out.shape[1] // H
    out_rows = w_out.reshape(k_mid, halves, H).transpose(1, 0, 2).reshape(halves * k_mid, H)
    return jnp.concatenate([w_in, conv_rows, out_rows], axis=0)


def per_device(
    tokens,
    breaks,
    lengths,
    embed_table,
    break_vec,
    gain_in,
    gain_mid,
    gain_out,
    w_in,
    convolution_weight,
    w_out,
):
    local_rows = tokens.shape[1]
    complexes = tokens.shape[0]
    seq_place = lax.axis_index("seq")
    k_in = w_in.shape[1]
    k_mid = convolution_weight.shape[1]
    d_model = w_out.shape[2]
    halves = d_model // H
    n_slots = lax.axis_size("ylo") * lax.axis_size("x") * lax.axis_size("core")

    packed = jnp.stack(
        [pack_block(w_in[b], convolution_weight[b], w_out[b]) for b in range(BLOCKS)], axis=0
    )
    gathered = gather_weights(packed, n_slots)

    onehot = (tokens[:, :, None] == jnp.arange(VOCAB, dtype=jnp.int32)[None, None, :]).astype(
        jnp.float32
    )
    hidden_state = jnp.einsum(
        "cnv,vd->cnd",
        onehot,
        embed_table,
        precision=lax.Precision.HIGHEST,
        preferred_element_type=jnp.float32,
    )
    hidden_state = (
        hidden_state + breaks[:, :, None].astype(jnp.float32) * break_vec[None, None, :]
    ).astype(jnp.bfloat16)
    position = seq_place * local_rows + jnp.arange(local_rows, dtype=jnp.int32)
    valid_rows = ((position[None, :] >= 0) & (position[None, :] < lengths[:, None])).astype(
        jnp.float32
    )
    for block_number in range(BLOCKS):
        dilation_step = BASE_DILATION * 2**block_number
        reach_rows = KERNEL // 2 * dilation_step
        slab = gathered[:, block_number]
        in_full = slab[:, :k_in, :].reshape(n_slots * k_in, H)
        normed = jax.nn.gelu(
            layer_norm(hidden_state.astype(jnp.float32), gain_in[block_number]), approximate=False
        ).astype(jnp.bfloat16)
        padded_hidden = jnp.einsum(
            "cnd,dh->cnh", normed, in_full, preferred_element_type=jnp.float32
        )
        conv_input = (
            jax.nn.gelu(layer_norm(padded_hidden, gain_mid[block_number]), approximate=False)
            * valid_rows[:, :, None]
        ).astype(jnp.bfloat16)
        extended = extended_2(conv_input, (("seq", 1),), reach_rows)
        mixed = jnp.zeros((complexes, local_rows, H), jnp.float32)
        for tap in range(KERNEL):
            start = k_in + tap * k_mid
            tap_w = slab[:, start : start + k_mid, :].reshape(n_slots * k_mid, H)
            window = extended[:, tap * dilation_step : tap * dilation_step + local_rows]
            mixed = mixed + jnp.einsum(
                "cnh,hg->cng", window, tap_w, preferred_element_type=jnp.float32
            )
        activated = jax.nn.gelu(
            layer_norm(mixed, gain_out[block_number]), approximate=False
        ).astype(jnp.bfloat16)
        start = k_in + KERNEL * k_mid
        out_full = (
            slab[:, start : start + halves * k_mid, :]
            .reshape(n_slots, halves, k_mid, H)
            .transpose(0, 2, 1, 3)
            .reshape(n_slots * k_mid, d_model)
        )
        update = jnp.einsum(
            "cnh,hd->cnd", activated, out_full, preferred_element_type=jnp.float32
        )
        hidden_state = (hidden_state.astype(jnp.float32) + update).astype(jnp.bfloat16)
    return hidden_state


def solution(mesh):
    seq_size, roll_size = mesh.devices.shape
    devices = mesh.devices.reshape(seq_size, roll_size // 8, 4, 2)
    fine = Mesh(devices, ("seq",) + ROLL)
    placed = (
        P(ROLL, "seq"),
        P(ROLL, "seq"),
        P(ROLL),
        P(),
        P(),
        P(),
        P(),
        P(),
        P(None, ROLL, None),
        P(None, ROLL, None),
        P(None, ROLL, None),
    )
    return jax.shard_map(
        per_device, mesh=fine, in_specs=placed, out_specs=P(ROLL, "seq", None), check_vma=False
    )
```

```python
import functools

import jax
import numpy as np
import jax.numpy as jnp
from jax import lax
from jax.experimental import pallas as pl
from jax.experimental.pallas import tpu as pltpu
from jax.sharding import Mesh, PartitionSpec as P

H = 640
KERNEL = 5
VOCAB = 30
BLOCKS = 2
BASE_DILATION = 64
ROLL = ("ylo", "x", "core")
MESH = pl.DeviceIdType.MESH


def halo_kernel(reach, x_ref, zeros_ref, out_ref, send_sem, recv_sem, local_sem):
    n_seq = lax.axis_size("seq")
    seq_i = lax.axis_index("seq")
    ylo = lax.axis_index("ylo")
    x = lax.axis_index("x")
    c = lax.axis_index("core")
    rows = x_ref.shape[0]
    has_prev = seq_i > 0
    has_next = seq_i < n_seq - 1
    prev = (seq_i - 1, ylo, x, c)
    nxt = (seq_i + 1, ylo, x, c)

    barrier = pltpu.get_barrier_semaphore()

    n_peers = (seq_i + n_seq - 1) // n_seq + (2 * n_seq - 2 - seq_i) // n_seq

    @pl.when(has_prev)
    def _():
        pl.semaphore_signal(barrier, inc=1, device_id=prev, device_id_type=MESH)

    @pl.when(has_next)
    def _():
        pl.semaphore_signal(barrier, inc=1, device_id=nxt, device_id_type=MESH)

    pl.semaphore_wait(barrier, n_peers)

    to_next = pltpu.make_async_remote_copy(
        src_ref=x_ref.at[pl.ds(rows - reach, reach)],
        dst_ref=out_ref.at[pl.ds(0, reach)],
        send_sem=send_sem.at[0],
        recv_sem=recv_sem.at[0],
        device_id=nxt,
        device_id_type=MESH,
    )
    to_prev = pltpu.make_async_remote_copy(
        src_ref=x_ref.at[pl.ds(0, reach)],
        dst_ref=out_ref.at[pl.ds(rows + reach, reach)],
        send_sem=send_sem.at[1],
        recv_sem=recv_sem.at[1],
        device_id=prev,
        device_id_type=MESH,
    )
    from_prev = pltpu.make_async_remote_copy(
        src_ref=x_ref.at[pl.ds(rows - reach, reach)],
        dst_ref=out_ref.at[pl.ds(0, reach)],
        send_sem=send_sem.at[0],
        recv_sem=recv_sem.at[0],
        device_id=prev,
        device_id_type=MESH,
    )
    from_next = pltpu.make_async_remote_copy(
        src_ref=x_ref.at[pl.ds(0, reach)],
        dst_ref=out_ref.at[pl.ds(rows + reach, reach)],
        send_sem=send_sem.at[1],
        recv_sem=recv_sem.at[1],
        device_id=nxt,
        device_id_type=MESH,
    )
    middle = pltpu.make_async_copy(x_ref, out_ref.at[pl.ds(reach, rows)], local_sem.at[0])
    head = pltpu.make_async_copy(zeros_ref, out_ref.at[pl.ds(0, reach)], local_sem.at[1])
    tail = pltpu.make_async_copy(zeros_ref, out_ref.at[pl.ds(rows + reach, reach)], local_sem.at[2])

    @pl.when(has_next)
    def _():
        to_next.start()

    @pl.when(has_prev)
    def _():
        to_prev.start()

    middle.start()

    @pl.when(jnp.logical_not(has_prev))
    def _():
        head.start()

    @pl.when(jnp.logical_not(has_next))
    def _():
        tail.start()

    middle.wait()

    @pl.when(has_next)
    def _():
        to_next.wait_send()
        from_next.wait_recv()

    @pl.when(has_prev)
    def _():
        to_prev.wait_send()
        from_prev.wait_recv()

    @pl.when(jnp.logical_not(has_prev))
    def _():
        head.wait()

    @pl.when(jnp.logical_not(has_next))
    def _():
        tail.wait()


def extend_halo(x, reach, collective_id):
    rows, width = x.shape
    zeros = jnp.zeros((reach, width), x.dtype)
    any_spec = pl.BlockSpec(memory_space=pl.ANY)
    return pl.pallas_call(
        functools.partial(halo_kernel, reach),
        out_shape=jax.ShapeDtypeStruct((rows + 2 * reach, width), x.dtype),
        in_specs=[any_spec, any_spec],
        out_specs=any_spec,
        scratch_shapes=[
            pltpu.SemaphoreType.DMA((2,)),
            pltpu.SemaphoreType.DMA((2,)),
            pltpu.SemaphoreType.DMA((3,)),
        ],
        compiler_params=pltpu.CompilerParams(
            collective_id=collective_id, has_side_effects=True
        ),
    )(x, zeros)


def layer_norm(values, gain):
    center = jnp.mean(values, axis=-1, keepdims=True)
    spread = jnp.mean((values - center) ** 2, axis=-1, keepdims=True)
    return (values - center) * lax.rsqrt(spread + 1e-05) * gain


def norm_gelu_rows(hidden_ref, gain_ref, normed_ref):
    rows = 16
    gain = gain_ref[...]

    def body(i, carry):
        span = pl.ds(pl.multiple_of(i * rows, rows), rows)
        values = hidden_ref[span, :].astype(jnp.float32)
        t = layer_norm(values, gain)
        gelu = 0.5 * t * (1.0 + lax.erf(t * np.float32(np.sqrt(0.5))))
        normed_ref[span, :] = gelu.astype(normed_ref.dtype)
        return carry

    lax.fori_loop(0, hidden_ref.shape[0] // rows, body, 0)


def gather_kernel(w_in_ref, conv_ref, w_out_ref, hidden_ref, gain_ref, in_out, conv_out, w_out_out, normed_ref, send_sem, recv_sem, local_sem):
    n_x = lax.axis_size("x")
    k_in = w_in_ref.shape[1]
    k_mid = conv_ref.shape[1]
    seq_i = lax.axis_index("seq")
    ylo = lax.axis_index("ylo")
    x = lax.axis_index("x")
    c = lax.axis_index("core")
    z = seq_i // 2
    y = (seq_i % 2) * 2 + ylo
    other = 1 - ylo

    def slot(par, xx, cc):
        return (par * n_x + xx) * 2 + cc

    def y_dev(yy):
        return (z * 2 + yy // 2, yy % 2, x, c)

    x_right = lax.rem(x + 1, n_x)
    x_left = lax.rem(x + n_x - 1, n_x)
    x_far = lax.rem(x + 2, n_x)
    right = (seq_i, ylo, x_right, c)
    left = (seq_i, ylo, x_left, c)
    up = y_dev(lax.rem(y + 1, 4))
    down = y_dev(lax.rem(y + 3, 4))
    partner = (seq_i, ylo, x, 1 - c)

    barrier = pltpu.get_barrier_semaphore()
    for dev in (right, left, up, down, partner):
        pl.semaphore_signal(barrier, inc=1, device_id=dev, device_id_type=MESH)
    pl.semaphore_wait(barrier, 5)

    def pieces(s, b):
        rows_in = pl.ds(pl.multiple_of(s * k_in, 8), k_in)
        rows_mid = pl.ds(pl.multiple_of(s * k_mid, 8), k_mid)
        dst = [in_out.at[b, rows_in]]
        dst += [conv_out.at[b, k, rows_mid] for k in range(KERNEL)]
        dst += [w_out_out.at[b, rows_mid]]
        return dst

    def own_pieces(b):
        src = [w_in_ref.at[b]]
        src += [conv_ref.at[b, :, pl.ds(k * H, H)] for k in range(KERNEL)]
        src += [w_out_ref.at[b]]
        return src

    sends = []

    def send(s, b, dev, own=False):
        dst = pieces(s, b)
        src = own_pieces(b) if own else dst
        for i, (a, d) in enumerate(zip(src, dst)):
            cp = pltpu.make_async_remote_copy(
                src_ref=a,
                dst_ref=d,
                send_sem=send_sem.at[len(sends)],
                recv_sem=recv_sem.at[s, b, i],
                device_id=dev,
                device_id_type=MESH,
            )
            cp.start()
            sends.append(cp)

    def arrive(s, b, dev):
        for i, d in enumerate(pieces(s, b)):
            pltpu.make_async_remote_copy(
                src_ref=d,
                dst_ref=d,
                send_sem=send_sem.at[0],
                recv_sem=recv_sem.at[s, b, i],
                device_id=dev,
                device_id_type=MESH,
            ).wait_recv()

    me = slot(ylo, x, c)
    for h in range(2):
        send(me, h, right, own=True)
    for h in range(2):
        send(me, h, left, own=True)
    send(me, 0, up, own=True)
    send(me, 1, down, own=True)
    for h in range(2):
        send(me, h, partner, own=True)
    locals_ = []
    for h in range(2):
        for a, d in zip(own_pieces(h), pieces(me, h)):
            cp = pltpu.make_async_copy(a, d, local_sem.at[len(locals_)])
            cp.start()
            locals_.append(cp)

    norm_gelu_rows(hidden_ref, gain_ref, normed_ref)

    s_left = slot(ylo, x_left, c)
    s_right = slot(ylo, x_right, c)
    for h in range(2):
        arrive(s_left, h, left)
    send(s_left, 0, right)
    send(s_left, 0, up)
    send(s_left, 1, down)
    for h in range(2):
        arrive(s_right, h, right)
    send(s_right, 1, left)
    send(s_right, 0, up)
    send(s_right, 1, down)
    for s in (s_left, s_right):
        for h in range(2):
            send(s, h, partner)

    s_far = slot(ylo, x_far, c)
    arrive(s_far, 0, left)
    arrive(s_far, 1, right)
    send(s_far, 0, up)
    send(s_far, 1, down)
    for h in range(2):
        send(s_far, h, partner)

    for xx in (x, x_left, x_right, x_far):
        s = slot(other, xx, c)
        arrive(s, 0, down)
        arrive(s, 1, up)
        for h in range(2):
            send(s, h, partner)

    for par in (ylo, other):
        for xx in (x, x_left, x_right, x_far):
            s = slot(par, xx, 1 - c)
            for h in range(2):
                arrive(s, h, partner)
    for cp in sends:
        cp.wait_send()
    for cp in locals_:
        cp.wait()


def gather_weights(w_in, conv, w_out, hidden, gain, n_slots):
    blocks, k_in, _ = w_in.shape
    k_mid = conv.shape[1]
    d_model = w_out.shape[2]
    n_pieces = KERNEL + 2
    any_spec = pl.BlockSpec(memory_space=pl.ANY)
    vmem_spec = pl.BlockSpec(memory_space=pltpu.VMEM)
    return pl.pallas_call(
        gather_kernel,
        out_shape=(
            jax.ShapeDtypeStruct((blocks, n_slots * k_in, H), w_in.dtype),
            jax.ShapeDtypeStruct((blocks, KERNEL, n_slots * k_mid, H), conv.dtype),
            jax.ShapeDtypeStruct((blocks, n_slots * k_mid, d_model), w_out.dtype),
            jax.ShapeDtypeStruct(hidden.shape, jnp.bfloat16),
        ),
        in_specs=[any_spec] * 3 + [vmem_spec] * 2,
        out_specs=(any_spec,) * 3 + (vmem_spec,),
        scratch_shapes=[
            pltpu.SemaphoreType.DMA((30 * n_pieces,)),
            pltpu.SemaphoreType.DMA((n_slots, blocks, n_pieces)),
            pltpu.SemaphoreType.DMA((blocks * n_pieces,)),
        ],
        compiler_params=pltpu.CompilerParams(collective_id=0, has_side_effects=True),
    )(w_in, conv, w_out, hidden, gain)


def per_device(
    tokens,
    breaks,
    lengths,
    embed_table,
    break_vec,
    gain_in,
    gain_mid,
    gain_out,
    w_in,
    convolution_weight,
    w_out,
):
    local_rows = tokens.shape[1]
    complexes = tokens.shape[0]
    seq_place = lax.axis_index("seq")
    k_in = w_in.shape[1]
    k_mid = convolution_weight.shape[1]
    d_model = w_out.shape[2]
    halves = d_model // H
    n_slots = lax.axis_size("ylo") * lax.axis_size("x") * lax.axis_size("core")


    onehot = (tokens[:, :, None] == jnp.arange(VOCAB, dtype=jnp.int32)[None, None, :]).astype(
        jnp.float32
    )
    hidden_state = jnp.einsum(
        "cnv,vd->cnd",
        onehot,
        embed_table,
        precision=lax.Precision.HIGHEST,
        preferred_element_type=jnp.float32,
    )
    hidden_state = (
        hidden_state + breaks[:, :, None].astype(jnp.float32) * break_vec[None, None, :]
    ).astype(jnp.bfloat16)
    in_all, conv_all, out_all, normed_first = gather_weights(
        w_in, convolution_weight, w_out, hidden_state[0], gain_in[0:1], n_slots
    )
    position = seq_place * local_rows + jnp.arange(local_rows, dtype=jnp.int32)
    valid_rows = ((position[None, :] >= 0) & (position[None, :] < lengths[:, None])).astype(
        jnp.float32
    )
    for block_number in range(BLOCKS):
        dilation_step = BASE_DILATION * 2**block_number
        reach_rows = KERNEL // 2 * dilation_step
        in_full = in_all[block_number]
        if block_number == 0:
            normed = normed_first.reshape(hidden_state.shape)
        else:
            normed = jax.nn.gelu(
                layer_norm(hidden_state.astype(jnp.float32), gain_in[block_number]),
                approximate=False,
            ).astype(jnp.bfloat16)
            normed = lax.optimization_barrier(normed)
        padded_hidden = jnp.einsum(
            "cnd,dh->cnh", normed, in_full, preferred_element_type=jnp.float32
        )
        conv_input = (
            jax.nn.gelu(layer_norm(padded_hidden, gain_mid[block_number]), approximate=False)
            * valid_rows[:, :, None]
        ).astype(jnp.bfloat16)
        extended = extend_halo(conv_input[0], reach_rows, 1 + block_number)[None]
        mixed = jnp.zeros((complexes, local_rows, H), jnp.float32)
        for tap in range(KERNEL):
            tap_w = conv_all[block_number, tap]
            window = extended[:, tap * dilation_step : tap * dilation_step + local_rows]
            mixed = mixed + jnp.einsum(
                "cnh,hg->cng", window, tap_w, preferred_element_type=jnp.float32
            )
        activated = jax.nn.gelu(
            layer_norm(mixed, gain_out[block_number]), approximate=False
        ).astype(jnp.bfloat16)
        activated = lax.optimization_barrier(activated)
        out_full = out_all[block_number]
        update = jnp.einsum(
            "cnh,hd->cnd", activated, out_full, preferred_element_type=jnp.float32
        )
        hidden_state = (hidden_state.astype(jnp.float32) + update).astype(jnp.bfloat16)
    return hidden_state


def solution(mesh):
    seq_size, roll_size = mesh.devices.shape
    devices = mesh.devices.reshape(seq_size, roll_size // 8, 4, 2)
    fine = Mesh(devices, ("seq",) + ROLL)
    placed = (
        P(ROLL, "seq"),
        P(ROLL, "seq"),
        P(ROLL),
        P(),
        P(),
        P(),
        P(),
        P(),
        P(None, ROLL, None),
        P(None, ROLL, None),
        P(None, ROLL, None),
    )
    return jax.shard_map(
        per_device, mesh=fine, in_specs=placed, out_specs=P(ROLL, "seq", None), check_vma=False
    )
```

```python
import functools

import jax
import numpy as np
import jax.numpy as jnp
from jax import lax
from jax.experimental import pallas as pl
from jax.experimental.pallas import tpu as pltpu
from jax.sharding import Mesh, PartitionSpec as P

H = 640
KERNEL = 5
VOCAB = 30
BLOCKS = 2
BASE_DILATION = 64
ROLL = ("ylo", "x", "core")
MESH = pl.DeviceIdType.MESH


def halo_kernel(reach, x_ref, out_ref, send_sem, recv_sem):
    n_seq = lax.axis_size("seq")
    seq_i = lax.axis_index("seq")
    ylo = lax.axis_index("ylo")
    x = lax.axis_index("x")
    c = lax.axis_index("core")
    rows = x_ref.shape[0]
    has_prev = seq_i > 0
    has_next = seq_i < n_seq - 1
    prev = (seq_i - 1, ylo, x, c)
    nxt = (seq_i + 1, ylo, x, c)

    barrier = pltpu.get_barrier_semaphore()
    n_peers = (seq_i + n_seq - 1) // n_seq + (2 * n_seq - 2 - seq_i) // n_seq

    @pl.when(has_prev)
    def _():
        pl.semaphore_signal(barrier, inc=1, device_id=prev, device_id_type=MESH)

    @pl.when(has_next)
    def _():
        pl.semaphore_signal(barrier, inc=1, device_id=nxt, device_id_type=MESH)

    pl.semaphore_wait(barrier, n_peers)

    head = out_ref.at[pl.ds(0, reach)]
    tail = out_ref.at[pl.ds(rows + reach, reach)]
    to_next = pltpu.make_async_remote_copy(
        src_ref=x_ref.at[pl.ds(rows - reach, reach)],
        dst_ref=head,
        send_sem=send_sem.at[0],
        recv_sem=recv_sem.at[0],
        device_id=nxt,
        device_id_type=MESH,
    )
    to_prev = pltpu.make_async_remote_copy(
        src_ref=x_ref.at[pl.ds(0, reach)],
        dst_ref=tail,
        send_sem=send_sem.at[1],
        recv_sem=recv_sem.at[1],
        device_id=prev,
        device_id_type=MESH,
    )
    from_prev = pltpu.make_async_remote_copy(
        src_ref=x_ref.at[pl.ds(rows - reach, reach)],
        dst_ref=head,
        send_sem=send_sem.at[0],
        recv_sem=recv_sem.at[0],
        device_id=prev,
        device_id_type=MESH,
    )
    from_next = pltpu.make_async_remote_copy(
        src_ref=x_ref.at[pl.ds(0, reach)],
        dst_ref=tail,
        send_sem=send_sem.at[1],
        recv_sem=recv_sem.at[1],
        device_id=nxt,
        device_id_type=MESH,
    )

    @pl.when(has_next)
    def _():
        to_next.start()

    @pl.when(has_prev)
    def _():
        to_prev.start()

    out_ref[pl.ds(reach, rows), :] = x_ref[...]

    @pl.when(jnp.logical_not(has_prev))
    def _():
        head[...] = jnp.zeros(head.shape, head.dtype)

    @pl.when(jnp.logical_not(has_next))
    def _():
        tail[...] = jnp.zeros(tail.shape, tail.dtype)

    @pl.when(has_next)
    def _():
        to_next.wait_send()
        from_next.wait_recv()

    @pl.when(has_prev)
    def _():
        to_prev.wait_send()
        from_prev.wait_recv()


def extend_halo(x, reach, collective_id):
    rows, width = x.shape
    vmem_spec = pl.BlockSpec(memory_space=pltpu.VMEM)
    return pl.pallas_call(
        functools.partial(halo_kernel, reach),
        out_shape=jax.ShapeDtypeStruct((rows + 2 * reach, width), x.dtype),
        in_specs=[vmem_spec],
        out_specs=vmem_spec,
        scratch_shapes=[
            pltpu.SemaphoreType.DMA((2,)),
            pltpu.SemaphoreType.DMA((2,)),
        ],
        compiler_params=pltpu.CompilerParams(
            collective_id=collective_id, has_side_effects=True
        ),
    )(x)


def layer_norm(values, gain):
    center = jnp.mean(values, axis=-1, keepdims=True)
    spread = jnp.mean((values - center) ** 2, axis=-1, keepdims=True)
    return (values - center) * lax.rsqrt(spread + 1e-05) * gain


def norm_gelu_rows(hidden_ref, gain_ref, normed_ref):
    rows = 16
    gain = gain_ref[...]

    def body(i, carry):
        span = pl.ds(pl.multiple_of(i * rows, rows), rows)
        values = hidden_ref[span, :].astype(jnp.float32)
        t = layer_norm(values, gain)
        gelu = 0.5 * t * (1.0 + lax.erf(t * np.float32(np.sqrt(0.5))))
        normed_ref[span, :] = gelu.astype(normed_ref.dtype)
        return carry

    lax.fori_loop(0, hidden_ref.shape[0] // rows, body, 0)


def gather_kernel(w_in_ref, conv_ref, w_out_ref, hidden_ref, gain_ref, in_out, conv_out, w_out_out, normed_ref, send_sem, recv_sem, local_sem):
    n_x = lax.axis_size("x")
    k_in = w_in_ref.shape[1]
    k_mid = conv_ref.shape[1]
    seq_i = lax.axis_index("seq")
    ylo = lax.axis_index("ylo")
    x = lax.axis_index("x")
    c = lax.axis_index("core")
    z = seq_i // 2
    y = (seq_i % 2) * 2 + ylo
    other = 1 - ylo

    def slot(par, xx, cc):
        return (par * n_x + xx) * 2 + cc

    def y_dev(yy):
        return (z * 2 + yy // 2, yy % 2, x, c)

    x_right = lax.rem(x + 1, n_x)
    x_left = lax.rem(x + n_x - 1, n_x)
    x_far = lax.rem(x + 2, n_x)
    right = (seq_i, ylo, x_right, c)
    left = (seq_i, ylo, x_left, c)
    up = y_dev(lax.rem(y + 1, 4))
    down = y_dev(lax.rem(y + 3, 4))
    partner = (seq_i, ylo, x, 1 - c)

    barrier = pltpu.get_barrier_semaphore()
    for dev in (right, left, up, down, partner):
        pl.semaphore_signal(barrier, inc=1, device_id=dev, device_id_type=MESH)
    pl.semaphore_wait(barrier, 5)

    def pieces(s, b):
        rows_in = pl.ds(pl.multiple_of(s * k_in, 8), k_in)
        rows_mid = pl.ds(pl.multiple_of(s * k_mid, 8), k_mid)
        dst = [in_out.at[b, rows_in]]
        dst += [conv_out.at[b, k, rows_mid] for k in range(KERNEL)]
        dst += [w_out_out.at[b, rows_mid]]
        return dst

    def own_pieces(b):
        src = [w_in_ref.at[b]]
        src += [conv_ref.at[b, :, pl.ds(k * H, H)] for k in range(KERNEL)]
        src += [w_out_ref.at[b]]
        return src

    sends = []

    def send(s, b, dev, own=False):
        dst = pieces(s, b)
        src = own_pieces(b) if own else dst
        for i, (a, d) in enumerate(zip(src, dst)):
            cp = pltpu.make_async_remote_copy(
                src_ref=a,
                dst_ref=d,
                send_sem=send_sem.at[len(sends)],
                recv_sem=recv_sem.at[s, b, i],
                device_id=dev,
                device_id_type=MESH,
            )
            cp.start()
            sends.append(cp)

    def arrive(s, b, dev):
        for i, d in enumerate(pieces(s, b)):
            pltpu.make_async_remote_copy(
                src_ref=d,
                dst_ref=d,
                send_sem=send_sem.at[0],
                recv_sem=recv_sem.at[s, b, i],
                device_id=dev,
                device_id_type=MESH,
            ).wait_recv()

    me = slot(ylo, x, c)
    for h in range(2):
        send(me, h, right, own=True)
    for h in range(2):
        send(me, h, left, own=True)
    send(me, 0, up, own=True)
    send(me, 1, down, own=True)
    for h in range(2):
        send(me, h, partner, own=True)
    locals_ = []
    for h in range(2):
        for a, d in zip(own_pieces(h), pieces(me, h)):
            cp = pltpu.make_async_copy(a, d, local_sem.at[len(locals_)])
            cp.start()
            locals_.append(cp)

    norm_gelu_rows(hidden_ref, gain_ref, normed_ref)

    s_left = slot(ylo, x_left, c)
    s_right = slot(ylo, x_right, c)
    for h in range(2):
        arrive(s_left, h, left)
    send(s_left, 0, right)
    send(s_left, 0, up)
    send(s_left, 1, down)
    for h in range(2):
        arrive(s_right, h, right)
    send(s_right, 1, left)
    send(s_right, 0, up)
    send(s_right, 1, down)
    for s in (s_left, s_right):
        for h in range(2):
            send(s, h, partner)

    s_far = slot(ylo, x_far, c)
    arrive(s_far, 0, left)
    arrive(s_far, 1, right)
    send(s_far, 0, up)
    send(s_far, 1, down)
    for h in range(2):
        send(s_far, h, partner)

    for xx in (x, x_left, x_right, x_far):
        s = slot(other, xx, c)
        arrive(s, 0, down)
        arrive(s, 1, up)
        for h in range(2):
            send(s, h, partner)

    for par in (ylo, other):
        for xx in (x, x_left, x_right, x_far):
            s = slot(par, xx, 1 - c)
            for h in range(2):
                arrive(s, h, partner)
    for cp in sends:
        cp.wait_send()
    for cp in locals_:
        cp.wait()


def gather_weights(w_in, conv, w_out, hidden, gain, n_slots):
    blocks, k_in, _ = w_in.shape
    k_mid = conv.shape[1]
    d_model = w_out.shape[2]
    n_pieces = KERNEL + 2
    any_spec = pl.BlockSpec(memory_space=pl.ANY)
    vmem_spec = pl.BlockSpec(memory_space=pltpu.VMEM)
    return pl.pallas_call(
        gather_kernel,
        out_shape=(
            jax.ShapeDtypeStruct((blocks, n_slots * k_in, H), w_in.dtype),
            jax.ShapeDtypeStruct((blocks, KERNEL, n_slots * k_mid, H), conv.dtype),
            jax.ShapeDtypeStruct((blocks, n_slots * k_mid, d_model), w_out.dtype),
            jax.ShapeDtypeStruct(hidden.shape, jnp.bfloat16),
        ),
        in_specs=[any_spec] * 3 + [vmem_spec] * 2,
        out_specs=(any_spec,) * 3 + (vmem_spec,),
        scratch_shapes=[
            pltpu.SemaphoreType.DMA((30 * n_pieces,)),
            pltpu.SemaphoreType.DMA((n_slots, blocks, n_pieces)),
            pltpu.SemaphoreType.DMA((blocks * n_pieces,)),
        ],
        compiler_params=pltpu.CompilerParams(collective_id=0, has_side_effects=True),
    )(w_in, conv, w_out, hidden, gain)


def per_device(
    tokens,
    breaks,
    lengths,
    embed_table,
    break_vec,
    gain_in,
    gain_mid,
    gain_out,
    w_in,
    convolution_weight,
    w_out,
):
    local_rows = tokens.shape[1]
    complexes = tokens.shape[0]
    seq_place = lax.axis_index("seq")
    k_in = w_in.shape[1]
    k_mid = convolution_weight.shape[1]
    d_model = w_out.shape[2]
    halves = d_model // H
    n_slots = lax.axis_size("ylo") * lax.axis_size("x") * lax.axis_size("core")


    onehot = (tokens[:, :, None] == jnp.arange(VOCAB, dtype=jnp.int32)[None, None, :]).astype(
        jnp.float32
    )
    hidden_state = jnp.einsum(
        "cnv,vd->cnd",
        onehot,
        embed_table,
        precision=lax.Precision.HIGHEST,
        preferred_element_type=jnp.float32,
    )
    hidden_state = (
        hidden_state + breaks[:, :, None].astype(jnp.float32) * break_vec[None, None, :]
    ).astype(jnp.bfloat16)
    in_all, conv_all, out_all, normed_first = gather_weights(
        w_in, convolution_weight, w_out, hidden_state[0], gain_in[0:1], n_slots
    )
    position = seq_place * local_rows + jnp.arange(local_rows, dtype=jnp.int32)
    valid_rows = ((position[None, :] >= 0) & (position[None, :] < lengths[:, None])).astype(
        jnp.float32
    )
    for block_number in range(BLOCKS):
        dilation_step = BASE_DILATION * 2**block_number
        reach_rows = KERNEL // 2 * dilation_step
        in_full = in_all[block_number]
        if block_number == 0:
            normed = normed_first.reshape(hidden_state.shape)
        else:
            normed = jax.nn.gelu(
                layer_norm(hidden_state.astype(jnp.float32), gain_in[block_number]),
                approximate=False,
            ).astype(jnp.bfloat16)
            normed = lax.optimization_barrier(normed)
        padded_hidden = jnp.einsum(
            "cnd,dh->cnh", normed, in_full, preferred_element_type=jnp.float32
        )
        conv_input = (
            jax.nn.gelu(layer_norm(padded_hidden, gain_mid[block_number]), approximate=False)
            * valid_rows[:, :, None]
        ).astype(jnp.bfloat16)
        extended = extend_halo(conv_input[0], reach_rows, 1 + block_number)[None]
        mixed = jnp.zeros((complexes, local_rows, H), jnp.float32)
        for tap in range(KERNEL):
            tap_w = conv_all[block_number, tap]
            window = extended[:, tap * dilation_step : tap * dilation_step + local_rows]
            mixed = mixed + jnp.einsum(
                "cnh,hg->cng", window, tap_w, preferred_element_type=jnp.float32
            )
        activated = jax.nn.gelu(
            layer_norm(mixed, gain_out[block_number]), approximate=False
        ).astype(jnp.bfloat16)
        activated = lax.optimization_barrier(activated)
        out_full = out_all[block_number]
        update = jnp.einsum(
            "cnh,hd->cnd", activated, out_full, preferred_element_type=jnp.float32
        )
        hidden_state = (hidden_state.astype(jnp.float32) + update).astype(jnp.bfloat16)
    return hidden_state


def solution(mesh):
    seq_size, roll_size = mesh.devices.shape
    devices = mesh.devices.reshape(seq_size, roll_size // 8, 4, 2)
    fine = Mesh(devices, ("seq",) + ROLL)
    placed = (
        P(ROLL, "seq"),
        P(ROLL, "seq"),
        P(ROLL),
        P(),
        P(),
        P(),
        P(),
        P(),
        P(None, ROLL, None),
        P(None, ROLL, None),
        P(None, ROLL, None),
    )
    return jax.shard_map(
        per_device, mesh=fine, in_specs=placed, out_specs=P(ROLL, "seq", None), check_vma=False
    )
```

```python
import jax
import numpy as np
import jax.numpy as jnp
from jax import lax
from jax.experimental import pallas as pl
from jax.experimental.pallas import tpu as pltpu
from jax.sharding import Mesh, PartitionSpec as P

H = 640
KERNEL = 5
VOCAB = 30
BLOCKS = 2
BASE_DILATION = 64
ROLL = ("ylo", "x", "core")
MESH = pl.DeviceIdType.MESH


def extended_2(x, sides, width):
    for axis, dim in sides:
        size, length = (lax.axis_size(axis), x.shape[dim])
        up = [(i, (i + 1) % size) for i in range(size - 1)]
        down = [(j, i) for i, j in up]
        last = lax.slice_in_dim(x, length - width, length, axis=dim)
        initial = lax.slice_in_dim(x, 0, width, axis=dim)
        before = lax.ppermute(last, axis, up)
        after = lax.ppermute(initial, axis, down)
        x = jnp.concatenate([before, x, after], axis=dim)
    return x


def layer_norm(values, gain):
    center = jnp.mean(values, axis=-1, keepdims=True)
    spread = jnp.mean((values - center) ** 2, axis=-1, keepdims=True)
    return (values - center) * lax.rsqrt(spread + 1e-05) * gain


def embed_norm_rows(tok_ref, brk_ref, table_ref, bvec_ref, gain_ref, hidden_ref, normed_ref):
    rows = 16
    gain = gain_ref[...]
    bvec = bvec_ref[...]

    def body(i, carry):
        span = pl.ds(pl.multiple_of(i * rows, rows), rows)
        tok = tok_ref[span, :]
        picked = jnp.zeros((rows, table_ref.shape[1]), jnp.float32)
        for v in range(table_ref.shape[0]):
            picked = jnp.where(tok == v, table_ref[v : v + 1, :], picked)
        row = (picked + brk_ref[span, :].astype(jnp.float32) * bvec).astype(hidden_ref.dtype)
        hidden_ref[span, :] = row
        t = layer_norm(row.astype(jnp.float32), gain)
        gelu = 0.5 * t * (1.0 + lax.erf(t * np.float32(np.sqrt(0.5))))
        normed_ref[span, :] = gelu.astype(normed_ref.dtype)
        return carry

    lax.fori_loop(0, hidden_ref.shape[0] // rows, body, 0)


def gather_kernel(w_in_ref, conv_ref, w_out_ref, tok_ref, brk_ref, table_ref, bvec_ref, gain_ref, in_out, conv_out, w_out_out, hidden_ref, normed_ref, send_sem, recv_sem, local_sem):
    n_x = lax.axis_size("x")
    k_in = w_in_ref.shape[1]
    k_mid = conv_ref.shape[1]
    seq_i = lax.axis_index("seq")
    ylo = lax.axis_index("ylo")
    x = lax.axis_index("x")
    c = lax.axis_index("core")
    z = seq_i // 2
    y = (seq_i % 2) * 2 + ylo
    other = 1 - ylo

    def slot(par, xx, cc):
        return (par * n_x + xx) * 2 + cc

    def y_dev(yy):
        return (z * 2 + yy // 2, yy % 2, x, c)

    x_right = lax.rem(x + 1, n_x)
    x_left = lax.rem(x + n_x - 1, n_x)
    x_far = lax.rem(x + 2, n_x)
    right = (seq_i, ylo, x_right, c)
    left = (seq_i, ylo, x_left, c)
    up = y_dev(lax.rem(y + 1, 4))
    down = y_dev(lax.rem(y + 3, 4))
    partner = (seq_i, ylo, x, 1 - c)

    barrier = pltpu.get_barrier_semaphore()
    for dev in (right, left, up, down, partner):
        pl.semaphore_signal(barrier, inc=1, device_id=dev, device_id_type=MESH)
    pl.semaphore_wait(barrier, 5)

    def pieces(s, b):
        rows_in = pl.ds(pl.multiple_of(s * k_in, 8), k_in)
        rows_mid = pl.ds(pl.multiple_of(s * k_mid, 8), k_mid)
        dst = [in_out.at[b, rows_in]]
        dst += [conv_out.at[b, k, rows_mid] for k in range(KERNEL)]
        dst += [w_out_out.at[b, rows_mid]]
        return dst

    def own_pieces(b):
        src = [w_in_ref.at[b]]
        src += [conv_ref.at[b, :, pl.ds(k * H, H)] for k in range(KERNEL)]
        src += [w_out_ref.at[b]]
        return src

    sends = []

    def send(s, b, dev, own=False):
        dst = pieces(s, b)
        src = own_pieces(b) if own else dst
        for i, (a, d) in enumerate(zip(src, dst)):
            cp = pltpu.make_async_remote_copy(
                src_ref=a,
                dst_ref=d,
                send_sem=send_sem.at[len(sends)],
                recv_sem=recv_sem.at[s, b, i],
                device_id=dev,
                device_id_type=MESH,
            )
            cp.start()
            sends.append(cp)

    def arrive(s, b, dev):
        for i, d in enumerate(pieces(s, b)):
            pltpu.make_async_remote_copy(
                src_ref=d,
                dst_ref=d,
                send_sem=send_sem.at[0],
                recv_sem=recv_sem.at[s, b, i],
                device_id=dev,
                device_id_type=MESH,
            ).wait_recv()

    me = slot(ylo, x, c)
    for h in range(2):
        send(me, h, right, own=True)
    for h in range(2):
        send(me, h, left, own=True)
    send(me, 0, up, own=True)
    send(me, 1, down, own=True)
    for h in range(2):
        send(me, h, partner, own=True)
    locals_ = []
    for h in range(2):
        for a, d in zip(own_pieces(h), pieces(me, h)):
            cp = pltpu.make_async_copy(a, d, local_sem.at[len(locals_)])
            cp.start()
            locals_.append(cp)

    embed_norm_rows(tok_ref, brk_ref, table_ref, bvec_ref, gain_ref, hidden_ref, normed_ref)

    s_left = slot(ylo, x_left, c)
    s_right = slot(ylo, x_right, c)
    for h in range(2):
        arrive(s_left, h, left)
    send(s_left, 0, right)
    send(s_left, 0, up)
    send(s_left, 1, down)
    for h in range(2):
        arrive(s_right, h, right)
    send(s_right, 1, left)
    send(s_right, 0, up)
    send(s_right, 1, down)
    for s in (s_left, s_right):
        for h in range(2):
            send(s, h, partner)

    s_far = slot(ylo, x_far, c)
    arrive(s_far, 0, left)
    arrive(s_far, 1, right)
    send(s_far, 0, up)
    send(s_far, 1, down)
    for h in range(2):
        send(s_far, h, partner)

    for xx in (x, x_left, x_right, x_far):
        s = slot(other, xx, c)
        arrive(s, 0, down)
        arrive(s, 1, up)
        for h in range(2):
            send(s, h, partner)

    for par in (ylo, other):
        for xx in (x, x_left, x_right, x_far):
            s = slot(par, xx, 1 - c)
            for h in range(2):
                arrive(s, h, partner)
    for cp in sends:
        cp.wait_send()
    for cp in locals_:
        cp.wait()


def gather_weights(w_in, conv, w_out, tok, brk, table, bvec, gain, n_slots):
    blocks, k_in, _ = w_in.shape
    k_mid = conv.shape[1]
    d_model = w_out.shape[2]
    n_pieces = KERNEL + 2
    any_spec = pl.BlockSpec(memory_space=pl.ANY)
    vmem_spec = pl.BlockSpec(memory_space=pltpu.VMEM)
    return pl.pallas_call(
        gather_kernel,
        out_shape=(
            jax.ShapeDtypeStruct((blocks, n_slots * k_in, H), w_in.dtype),
            jax.ShapeDtypeStruct((blocks, KERNEL, n_slots * k_mid, H), conv.dtype),
            jax.ShapeDtypeStruct((blocks, n_slots * k_mid, d_model), w_out.dtype),
            jax.ShapeDtypeStruct((tok.shape[0], table.shape[1]), jnp.bfloat16),
            jax.ShapeDtypeStruct((tok.shape[0], table.shape[1]), jnp.bfloat16),
        ),
        in_specs=[vmem_spec] * 8,
        out_specs=(any_spec,) * 3 + (vmem_spec,) * 2,
        scratch_shapes=[
            pltpu.SemaphoreType.DMA((30 * n_pieces,)),
            pltpu.SemaphoreType.DMA((n_slots, blocks, n_pieces)),
            pltpu.SemaphoreType.DMA((blocks * n_pieces,)),
        ],
        compiler_params=pltpu.CompilerParams(collective_id=0, has_side_effects=True),
    )(w_in, conv, w_out, tok, brk, table, bvec, gain)


def per_device(
    tokens,
    breaks,
    lengths,
    embed_table,
    break_vec,
    gain_in,
    gain_mid,
    gain_out,
    w_in,
    convolution_weight,
    w_out,
):
    local_rows = tokens.shape[1]
    complexes = tokens.shape[0]
    seq_place = lax.axis_index("seq")
    k_in = w_in.shape[1]
    k_mid = convolution_weight.shape[1]
    d_model = w_out.shape[2]
    halves = d_model // H
    n_slots = lax.axis_size("ylo") * lax.axis_size("x") * lax.axis_size("core")


    in_all, conv_all, out_all, hidden_first, normed_first = gather_weights(
        w_in,
        convolution_weight,
        w_out,
        tokens.reshape(-1, 1),
        breaks.reshape(-1, 1),
        embed_table,
        break_vec.reshape(1, -1),
        gain_in[0:1],
        n_slots,
    )
    hidden_state = hidden_first.reshape(complexes, local_rows, -1)
    position = seq_place * local_rows + jnp.arange(local_rows, dtype=jnp.int32)
    valid_rows = ((position[None, :] >= 0) & (position[None, :] < lengths[:, None])).astype(
        jnp.float32
    )
    for block_number in range(BLOCKS):
        dilation_step = BASE_DILATION * 2**block_number
        reach_rows = KERNEL // 2 * dilation_step
        in_full = in_all[block_number]
        if block_number == 0:
            normed = normed_first.reshape(hidden_state.shape)
        else:
            normed = jax.nn.gelu(
                layer_norm(hidden_state.astype(jnp.float32), gain_in[block_number]),
                approximate=False,
            ).astype(jnp.bfloat16)
            normed = lax.optimization_barrier(normed)
        padded_hidden = jnp.einsum(
            "cnd,dh->cnh", normed, in_full, preferred_element_type=jnp.float32
        )
        conv_input = (
            jax.nn.gelu(layer_norm(padded_hidden, gain_mid[block_number]), approximate=False)
            * valid_rows[:, :, None]
        ).astype(jnp.bfloat16)
        extended = extended_2(conv_input, (("seq", 1),), reach_rows)
        mixed = jnp.zeros((complexes, local_rows, H), jnp.float32)
        for tap in range(KERNEL):
            tap_w = conv_all[block_number, tap]
            window = extended[:, tap * dilation_step : tap * dilation_step + local_rows]
            mixed = mixed + jnp.einsum(
                "cnh,hg->cng", window, tap_w, preferred_element_type=jnp.float32
            )
        activated = jax.nn.gelu(
            layer_norm(mixed, gain_out[block_number]), approximate=False
        ).astype(jnp.bfloat16)
        activated = lax.optimization_barrier(activated)
        out_full = out_all[block_number]
        update = jnp.einsum(
            "cnh,hd->cnd", activated, out_full, preferred_element_type=jnp.float32
        )
        hidden_state = (hidden_state.astype(jnp.float32) + update).astype(jnp.bfloat16)
    return hidden_state


def solution(mesh):
    seq_size, roll_size = mesh.devices.shape
    devices = mesh.devices.reshape(seq_size, roll_size // 8, 4, 2)
    fine = Mesh(devices, ("seq",) + ROLL)
    placed = (
        P(ROLL, "seq"),
        P(ROLL, "seq"),
        P(ROLL),
        P(),
        P(),
        P(),
        P(),
        P(),
        P(None, ROLL, None),
        P(None, ROLL, None),
        P(None, ROLL, None),
    )
    return jax.shard_map(
        per_device, mesh=fine, in_specs=placed, out_specs=P(ROLL, "seq", None), check_vma=False
    )
```

```python
import functools

import jax
import numpy as np
import jax.numpy as jnp
from jax import lax
from jax.experimental import pallas as pl
from jax.experimental.pallas import tpu as pltpu
from jax.sharding import Mesh, PartitionSpec as P

H = 640
KERNEL = 5
VOCAB = 30
BLOCKS = 2
BASE_DILATION = 64
ROLL = ("ylo", "x", "core")
MESH = pl.DeviceIdType.MESH


def extended_2(x, sides, width):
    for axis, dim in sides:
        size, length = (lax.axis_size(axis), x.shape[dim])
        up = [(i, (i + 1) % size) for i in range(size - 1)]
        down = [(j, i) for i, j in up]
        last = lax.slice_in_dim(x, length - width, length, axis=dim)
        initial = lax.slice_in_dim(x, 0, width, axis=dim)
        before = lax.ppermute(last, axis, up)
        after = lax.ppermute(initial, axis, down)
        x = jnp.concatenate([before, x, after], axis=dim)
    return x


def layer_norm(values, gain):
    center = jnp.mean(values, axis=-1, keepdims=True)
    spread = jnp.mean((values - center) ** 2, axis=-1, keepdims=True)
    return (values - center) * lax.rsqrt(spread + 1e-05) * gain


def embed_norm_rows(tok_ref, brk_ref, table_ref, bvec_ref, gain_ref, rows_ref, hidden_ref, normed_ref):
    bvec = bvec_ref[...]

    def fill(r, carry):
        picked = table_ref[pl.ds(tok_ref[r], 1), :]
        rows_ref[pl.ds(r, 1), :] = picked + brk_ref[r].astype(jnp.float32) * bvec[None, :]
        return carry

    lax.fori_loop(0, hidden_ref.shape[0], fill, 0)
    rows = 16
    gain = gain_ref[0, :]

    def body(i, carry):
        span = pl.ds(pl.multiple_of(i * rows, rows), rows)
        row = rows_ref[span, :].astype(hidden_ref.dtype)
        hidden_ref[span, :] = row
        t = layer_norm(row.astype(jnp.float32), gain[None, :])
        gelu = 0.5 * t * (1.0 + lax.erf(t * np.float32(np.sqrt(0.5))))
        normed_ref[span, :] = gelu.astype(normed_ref.dtype)
        return carry

    lax.fori_loop(0, hidden_ref.shape[0] // rows, body, 0)


def norm_gelu_kernel(block, hidden_ref, gain_ref, normed_ref):
    rows = 16
    gain = gain_ref[block, :]

    def body(i, carry):
        span = pl.ds(pl.multiple_of(i * rows, rows), rows)
        t = layer_norm(hidden_ref[span, :].astype(jnp.float32), gain[None, :])
        gelu = 0.5 * t * (1.0 + lax.erf(t * np.float32(np.sqrt(0.5))))
        normed_ref[span, :] = gelu.astype(normed_ref.dtype)
        return carry

    lax.fori_loop(0, hidden_ref.shape[0] // rows, body, 0)


def norm_gelu(hidden, gains, block):
    vmem_spec = pl.BlockSpec(memory_space=pltpu.VMEM)
    return pl.pallas_call(
        functools.partial(norm_gelu_kernel, block),
        out_shape=jax.ShapeDtypeStruct(hidden.shape, jnp.bfloat16),
        in_specs=[vmem_spec, vmem_spec],
        out_specs=vmem_spec,
    )(hidden, gains)


def gather_kernel(w_in_ref, conv_ref, w_out_ref, tok_ref, brk_ref, table_ref, bvec_ref, gain_ref, in_out, conv_out, w_out_out, hidden_ref, normed_ref, send_sem, recv_sem, local_sem, rows_ref):
    n_x = lax.axis_size("x")
    k_in = w_in_ref.shape[1]
    k_mid = conv_ref.shape[1]
    seq_i = lax.axis_index("seq")
    ylo = lax.axis_index("ylo")
    x = lax.axis_index("x")
    c = lax.axis_index("core")
    z = seq_i // 2
    y = (seq_i % 2) * 2 + ylo
    other = 1 - ylo

    def slot(par, xx, cc):
        return (par * n_x + xx) * 2 + cc

    def y_dev(yy):
        return (z * 2 + yy // 2, yy % 2, x, c)

    x_right = lax.rem(x + 1, n_x)
    x_left = lax.rem(x + n_x - 1, n_x)
    x_far = lax.rem(x + 2, n_x)
    right = (seq_i, ylo, x_right, c)
    left = (seq_i, ylo, x_left, c)
    up = y_dev(lax.rem(y + 1, 4))
    down = y_dev(lax.rem(y + 3, 4))
    partner = (seq_i, ylo, x, 1 - c)

    barrier = pltpu.get_barrier_semaphore()
    for dev in (right, left, up, down, partner):
        pl.semaphore_signal(barrier, inc=1, device_id=dev, device_id_type=MESH)
    pl.semaphore_wait(barrier, 5)

    def pieces(s, b):
        rows_in = pl.ds(pl.multiple_of(s * k_in, 8), k_in)
        rows_mid = pl.ds(pl.multiple_of(s * k_mid, 8), k_mid)
        dst = [in_out.at[b, rows_in]]
        dst += [conv_out.at[b, k, rows_mid] for k in range(KERNEL)]
        dst += [w_out_out.at[b, rows_mid]]
        return dst

    def own_pieces(b):
        src = [w_in_ref.at[b]]
        src += [conv_ref.at[b, :, pl.ds(k * H, H)] for k in range(KERNEL)]
        src += [w_out_ref.at[b]]
        return src

    sends = []

    def send(s, b, dev, own=False):
        dst = pieces(s, b)
        src = own_pieces(b) if own else dst
        for i, (a, d) in enumerate(zip(src, dst)):
            cp = pltpu.make_async_remote_copy(
                src_ref=a,
                dst_ref=d,
                send_sem=send_sem.at[len(sends)],
                recv_sem=recv_sem.at[s, b, i],
                device_id=dev,
                device_id_type=MESH,
            )
            cp.start()
            sends.append(cp)

    def arrive(s, b, dev):
        for i, d in enumerate(pieces(s, b)):
            pltpu.make_async_remote_copy(
                src_ref=d,
                dst_ref=d,
                send_sem=send_sem.at[0],
                recv_sem=recv_sem.at[s, b, i],
                device_id=dev,
                device_id_type=MESH,
            ).wait_recv()

    me = slot(ylo, x, c)
    for h in range(2):
        send(me, h, right, own=True)
        send(me, h, left, own=True)
    send(me, 0, up, own=True)
    send(me, 1, down, own=True)
    for h in range(2):
        send(me, h, partner, own=True)
    locals_ = []
    for h in range(2):
        for a, d in zip(own_pieces(h), pieces(me, h)):
            cp = pltpu.make_async_copy(a, d, local_sem.at[len(locals_)])
            cp.start()
            locals_.append(cp)

    embed_norm_rows(tok_ref, brk_ref, table_ref, bvec_ref, gain_ref, rows_ref, hidden_ref, normed_ref)

    s_left = slot(ylo, x_left, c)
    s_right = slot(ylo, x_right, c)
    arrive(s_left, 0, left)
    send(s_left, 0, right)
    send(s_left, 0, up)
    send(s_left, 0, partner)
    arrive(s_right, 0, right)
    send(s_right, 0, up)
    send(s_right, 0, partner)
    arrive(s_left, 1, left)
    send(s_left, 1, down)
    send(s_left, 1, partner)
    arrive(s_right, 1, right)
    send(s_right, 1, left)
    send(s_right, 1, down)
    send(s_right, 1, partner)

    s_far = slot(ylo, x_far, c)
    arrive(s_far, 0, left)
    arrive(s_far, 1, right)
    send(s_far, 0, up)
    send(s_far, 1, down)
    for h in range(2):
        send(s_far, h, partner)

    for xx in (x, x_left, x_right, x_far):
        s = slot(other, xx, c)
        arrive(s, 0, down)
        arrive(s, 1, up)
        for h in range(2):
            send(s, h, partner)

    for par in (ylo, other):
        for xx in (x, x_left, x_right, x_far):
            s = slot(par, xx, 1 - c)
            for h in range(2):
                arrive(s, h, partner)
    for cp in sends:
        cp.wait_send()
    for cp in locals_:
        cp.wait()


def gather_weights(w_in, conv, w_out, tok, brk, table, bvec, gain, n_slots):
    blocks, k_in, _ = w_in.shape
    k_mid = conv.shape[1]
    d_model = w_out.shape[2]
    n_pieces = KERNEL + 2
    any_spec = pl.BlockSpec(memory_space=pl.ANY)
    vmem_spec = pl.BlockSpec(memory_space=pltpu.VMEM)
    smem_spec = pl.BlockSpec(memory_space=pltpu.SMEM)
    return pl.pallas_call(
        gather_kernel,
        out_shape=(
            jax.ShapeDtypeStruct((blocks, n_slots * k_in, H), w_in.dtype),
            jax.ShapeDtypeStruct((blocks, KERNEL, n_slots * k_mid, H), conv.dtype),
            jax.ShapeDtypeStruct((blocks, n_slots * k_mid, d_model), w_out.dtype),
            jax.ShapeDtypeStruct((tok.shape[0], table.shape[1]), jnp.bfloat16),
            jax.ShapeDtypeStruct((tok.shape[0], table.shape[1]), jnp.bfloat16),
        ),
        in_specs=[any_spec] * 3 + [smem_spec] * 2 + [vmem_spec] * 3,
        out_specs=(any_spec,) * 3 + (vmem_spec,) * 2,
        scratch_shapes=[
            pltpu.SemaphoreType.DMA((30 * n_pieces,)),
            pltpu.SemaphoreType.DMA((n_slots, blocks, n_pieces)),
            pltpu.SemaphoreType.DMA((blocks * n_pieces,)),
            pltpu.VMEM((tok.shape[0], table.shape[1]), jnp.float32),
        ],
        compiler_params=pltpu.CompilerParams(collective_id=0, has_side_effects=True),
    )(w_in, conv, w_out, tok, brk, table, bvec, gain)


def per_device(
    tokens,
    breaks,
    lengths,
    embed_table,
    break_vec,
    gain_in,
    gain_mid,
    gain_out,
    w_in,
    convolution_weight,
    w_out,
):
    local_rows = tokens.shape[1]
    complexes = tokens.shape[0]
    seq_place = lax.axis_index("seq")
    k_in = w_in.shape[1]
    k_mid = convolution_weight.shape[1]
    d_model = w_out.shape[2]
    halves = d_model // H
    n_slots = lax.axis_size("ylo") * lax.axis_size("x") * lax.axis_size("core")


    in_all, conv_all, out_all, hidden_first, normed_first = gather_weights(
        w_in,
        convolution_weight,
        w_out,
        tokens.reshape(-1),
        breaks.reshape(-1),
        embed_table,
        break_vec,
        gain_in,
        n_slots,
    )
    hidden_state = hidden_first.reshape(complexes, local_rows, -1)
    position = seq_place * local_rows + jnp.arange(local_rows, dtype=jnp.int32)
    valid_rows = ((position[None, :] >= 0) & (position[None, :] < lengths[:, None])).astype(
        jnp.float32
    )
    for block_number in range(BLOCKS):
        dilation_step = BASE_DILATION * 2**block_number
        reach_rows = KERNEL // 2 * dilation_step
        in_full = in_all[block_number]
        if block_number == 0:
            normed = normed_first.reshape(hidden_state.shape)
        else:
            normed = norm_gelu(hidden_state[0], gain_in, block_number)[None]
        padded_hidden = jnp.einsum(
            "cnd,dh->cnh", normed, in_full, preferred_element_type=jnp.float32
        )
        conv_input = (
            jax.nn.gelu(layer_norm(padded_hidden, gain_mid[block_number]), approximate=False)
            * valid_rows[:, :, None]
        ).astype(jnp.bfloat16)
        extended = extended_2(conv_input, (("seq", 1),), reach_rows)
        mixed = jnp.zeros((complexes, local_rows, H), jnp.float32)
        for tap in range(KERNEL):
            tap_w = conv_all[block_number, tap]
            window = extended[:, tap * dilation_step : tap * dilation_step + local_rows]
            mixed = mixed + jnp.einsum(
                "cnh,hg->cng", window, tap_w, preferred_element_type=jnp.float32
            )
        activated = jax.nn.gelu(
            layer_norm(mixed, gain_out[block_number]), approximate=False
        ).astype(jnp.bfloat16)
        activated = lax.optimization_barrier(activated)
        out_full = out_all[block_number]
        update = jnp.einsum(
            "cnh,hd->cnd", activated, out_full, preferred_element_type=jnp.float32
        )
        hidden_state = (hidden_state.astype(jnp.float32) + update).astype(jnp.bfloat16)
    return hidden_state


def solution(mesh):
    seq_size, roll_size = mesh.devices.shape
    devices = mesh.devices.reshape(seq_size, roll_size // 8, 4, 2)
    fine = Mesh(devices, ("seq",) + ROLL)
    placed = (
        P(ROLL, "seq"),
        P(ROLL, "seq"),
        P(ROLL),
        P(),
        P(),
        P(),
        P(),
        P(),
        P(None, ROLL, None),
        P(None, ROLL, None),
        P(None, ROLL, None),
    )
    return jax.shard_map(
        per_device, mesh=fine, in_specs=placed, out_specs=P(ROLL, "seq", None), check_vma=False
    )
```
